32 devices in a mesh: row: 4 (over x, core), col: 8 (over z, y).
Axes of the slice: x: 2, y: 2, z: 4, core: 2. Of those that a mesh axis runs over, the one named last changes fastest.
Arguments:
- hamiltonian: float32 [8, 128, 1024], P(None, 'row', 'col'), may hold values from -73 to 73, as said below
Outputs:
- reduced: float32 [8, 128, 1024], P(None, 'row', 'col')
The draws below stay inside these ranges and needn't reach their ends.
Inputs may be any that keep to these rules, and one draw needn't show every extreme that they name: `hamiltonian`: the matrix A0 is symmetric.
All inputs are finite; a program needn't handle non-finite values.
Results may differ from the reference program's by a relative error of at most 0.0003.
Values sent between devices are 32-bit elements; how exact they have to be, the bound alone decides.
A program may use at most 64 MiB of HBM per device.

```python
import math
import jax
import jax.numpy as jnp
from jax import lax

B = 256
CW = 128
BLOCKS = 8
N = 1024


def draw_hamiltonian(key, part):
    first_key = jax.random.fold_in(key, 11)
    normal = jax.random.truncated_normal(first_key, -5.0, 5.0, (N, N), jnp.float32)
    matrix = (normal + normal.T) * math.sqrt(0.5)
    return matrix.reshape(BLOCKS, CW, N)


def setup_inputs(seed: int = 0) -> dict:
    splits = jax.random.split(jax.random.key(seed), 2)
    return {
        "hamiltonian": draw_hamiltonian(jax.random.fold_in(splits[1], 71), 0),
    }


HIGH = lax.Precision.HIGHEST

def matmul(left_side, right_side):
    return jnp.dot(left_side.astype(jnp.float32), right_side.astype(jnp.float32), precision=HIGH, preferred_element_type=jnp.float32)

def reflect_step(matrix, first_col):
    panel_cols = matrix[:, first_col:first_col + B]
    gram_matrix = matmul(panel_cols.T, panel_cols)
    factor = jnp.linalg.cholesky(gram_matrix)
    reflector = lax.linalg.triangular_solve(factor, panel_cols, left_side=False, lower=True, transpose_a=True)
    image = matmul(matrix.T, reflector)
    corner = matmul(reflector.T, image)
    corrected = 2.0 * image - 2.0 * matmul(reflector, corner)
    return matrix - matmul(reflector, corrected.T) - matmul(corrected, reflector.T)

def reference(hamiltonian):
    matrix = hamiltonian.reshape(N, N)
    for panel_index in range(2):
        matrix = reflect_step(matrix, panel_index * B)
    return matrix.reshape(BLOCKS, CW, N)
```

```python
import functools

import jax
import jax.numpy as jnp
from jax import lax
from jax.experimental import pallas as pl
from jax.experimental.pallas import tpu as pltpu
from jax.sharding import PartitionSpec as P

B = 256
NB = 32
GROUP = 16
LANES = 128
FAST_ORDER = 1024
HIGHEST = lax.Precision.HIGHEST
MESH = pl.DeviceIdType.MESH


def dot(left, right, dims, precision=HIGHEST):
    return lax.dot_general(
        left, right, (dims, ((), ())), precision=precision, preferred_element_type=jnp.float32
    )


def nn(left, right, precision=HIGHEST):
    return dot(left, right, ((1,), (0,)), precision)


def nt(left, right, precision=HIGHEST):
    return dot(left, right, ((1,), (1,)), precision)


def tn(left, right, precision=HIGHEST):
    return dot(left, right, ((0,), (0,)), precision)


def split3(value):
    high = value.astype(jnp.bfloat16)
    value = value - high.astype(jnp.float32)
    middle = value.astype(jnp.bfloat16)
    value = value - middle.astype(jnp.float32)
    return high, middle, value.astype(jnp.bfloat16)


def wide(value, times):
    return value if times == 1 else jnp.concatenate([value] * times, axis=1)


def inverse_factor(gram, work_ref, out_ref):
    size = gram.shape[0]
    work_ref[:, :size] = gram
    work_ref[:, size:] = (
        lax.broadcasted_iota(jnp.int32, (size, size), 0)
        == lax.broadcasted_iota(jnp.int32, (size, size), 1)
    ).astype(jnp.float32)
    out_ref[...] = jnp.zeros((size, size), jnp.float32)
    for low in range(0, size, NB):
        high = low + NB
        first = low // LANES * LANES
        last = size + -(-high // LANES) * LANES
        times = (last - first) // LANES
        rows = work_ref[low:high, first:last]
        done = []
        for start in range(0, NB, GROUP):
            lane = low + start - first
            height = NB - start
            columns = [
                jnp.broadcast_to(rows[:, lane + c : lane + c + 1], (height, LANES))
                for c in range(GROUP)
            ]
            ids = lax.broadcasted_iota(jnp.int32, (height, LANES), 0)
            pivots = jnp.ones((GROUP, LANES), jnp.float32)
            for k in range(GROUP):
                pivot = columns[k][k : k + 1]
                pivots = jnp.where(ids[:GROUP] == k, pivot, pivots)
                if start + k == NB - 1:
                    break
                below = jnp.where(ids > k, columns[k], 0.0) * (1.0 / pivot)
                for c in range(k + 1, GROUP):
                    columns[c] = columns[c] - below * columns[c][k : k + 1]
                rows = rows - wide(below, times) * rows[k : k + 1]
            done.append(rows[:GROUP] * wide(lax.rsqrt(pivots), times))
            rows = rows[GROUP:]
        rows = jnp.concatenate(done, axis=0)
        out_ref[low:high, : last - size] = rows[:, size - first :]
        if high < size:
            base = high // LANES * LANES
            a, b, c = split3(rows)
            right = jnp.concatenate([a, b, a, b, c, a], axis=0)
            left = jnp.concatenate([a, a, b, b, a, c], axis=0)[:, base - first : size - first]
            update = lax.dot_general(
                left, right, (((0,), (0,)), ((), ())), preferred_element_type=jnp.float32
            )
            work_ref[high:, first:last] -= update[high - base :]


def panels_kernel(
    h_ref, out_ref, a_ref, first_ref, rest_ref, work_ref, inverse_ref, second_ref, ut_ref, yt_ref, zt_ref, vt_ref,
    send_sems, recv_sems,
):
    blocks, strip, columns = h_ref.shape
    chain = lax.axis_size("col") // 2
    order = blocks * columns
    owners = B // columns
    others = blocks - owners
    kept = rest_ref.shape[3]
    row = lax.axis_index("row")
    col = lax.axis_index("col")
    x, core = row // 2, row % 2
    z, y = col // 2, col % 2
    over_x, over_y, over_core = ((1 - x) * 2 + core, col), (row, z * 2 + 1 - y), (x * 2 + 1 - core, col)

    def along_z(d):
        return (row, lax.rem(z + d, chain) * 2 + y)

    first_ref[col, x, core] = h_ref[:owners]

    @pl.when(col >= owners)
    def _():
        for i in range(kept):
            rest_ref[col, x, core, i] = h_ref[owners + lax.rem(col - owners + i, others)]

    barrier = pltpu.get_barrier_semaphore()
    peers = [over_x, over_y, over_core] + [along_z(d) for d in range(1, chain)]
    for peer in peers:
        pl.semaphore_signal(barrier, inc=1, device_id=peer, device_id_type=MESH)
    pl.semaphore_wait(barrier, len(peers))

    per_stage = 6 * chain
    buffers = (first_ref, rest_ref)
    sent = []

    def copy(stage, slot, d, piece, peer):
        index = stage * per_stage + slot * chain + d
        return pltpu.make_async_remote_copy(
            src_ref=piece,
            dst_ref=piece,
            send_sem=send_sems.at[index],
            recv_sem=recv_sems.at[index],
            device_id=peer,
            device_id_type=MESH,
        )

    def guarded(stage, source, action):
        if stage == 0:
            action()
        else:
            pl.when(source >= owners // 2)(action)

    def steps(stage, d, phase):
        ref = buffers[stage]
        half = ref.shape[3] // 2
        low, high = pl.ds(0, half), pl.ds(half, ref.shape[3] - half)
        source = lax.rem(z + chain - d, chain)
        pair = pl.ds(source * 2, 2)
        here, there = source * 2 + y, source * 2 + 1 - y
        every = pl.ds(0, 2)
        launches = []

        def arrive(slot, piece, peer):
            copy(stage, slot, d, piece, peer).wait_recv()

        def launch(slot, piece, peer):
            made = copy(stage, slot, d, piece, peer)
            made.start()
            launches.append((slot, piece, peer))

        def action():
            if phase == 0:
                if d > 0:
                    arrive(0, ref.at[here, x, core], along_z(d))
                launch(1, ref.at[here, x, core, low], over_y)
                launch(2, ref.at[here, x, core, high], over_x)
            elif phase == 1:
                arrive(1, ref.at[there, x, core, low], over_y)
                launch(3, ref.at[pair, x, core, low], over_x)
                arrive(2, ref.at[here, 1 - x, core, high], over_x)
                launch(4, ref.at[here, every, core, high], over_y)
            elif phase == 2:
                arrive(3, ref.at[pair, 1 - x, core, low], over_x)
                arrive(4, ref.at[there, every, core, high], over_y)
                launch(5, ref.at[pair, every, core], over_core)
            else:
                arrive(5, ref.at[pair, every, 1 - core], over_core)

        guarded(stage, source, action)
        for slot, piece, peer in launches:
            sent.append((stage, source, (slot, d, piece, peer)))

    def wave(stage, number):
        for phase in range(4):
            if 0 <= number - phase < chain:
                steps(stage, number - phase, phase)

    for stage in range(2):
        for d in range(1, chain):
            piece, peer = buffers[stage].at[col, x, core], along_z(d)

            def action(stage=stage, d=d, piece=piece, peer=peer):
                copy(stage, 0, d, piece, peer).start()

            guarded(stage, z, action)
            sent.append((stage, z, (0, d, piece, peer)))

    waves = chain + 3

    def whole(block):
        return block.reshape(-1, block.shape[-1])

    lag = 2
    for number in range(waves + lag):
        if number < waves:
            wave(0, number)
        if number >= lag:
            wave(1, number - lag)

    def place(block_row, block_col, block):
        a_ref[block_row, :, :, block_col * columns : (block_col + 1) * columns] = block.reshape(
            -1, strip, columns
        )

    for c in range(blocks):
        for i in range(owners):
            block = whole(first_ref[c, :, :, i].reshape(-1, strip, columns))
            place(i, c, block)
            if c >= owners:
                place(c, i, block.T)
    for c in range(owners, blocks):
        for i in range(kept):
            a = owners + (c - owners + i) % others
            block = whole(rest_ref[c, :, :, i].reshape(-1, strip, columns))
            place(a, c, block)
            if i > 0 and 2 * i != others:
                place(c, a, block.T)

    def matrix(low, high):
        return whole(whole(a_ref[low:high]).reshape(-1, order))

    panel = matrix(0, owners)
    inverse_factor(nt(panel, panel), work_ref, inverse_ref)
    tt = nn(panel, matrix(0, blocks))
    inverse = inverse_ref[...]
    ut_ref[...] = nn(inverse, panel)
    yt_ref[...] = nn(inverse, tt)
    later = slice(B, 2 * B)
    zt_ref[...] = matrix(owners, 2 * owners) - 2.0 * tn(ut_ref[:, later], yt_ref[...])
    zt = zt_ref[...]
    inverse_factor(nt(zt, zt), work_ref, second_ref)

    ut, yt = ut_ref[...], yt_ref[...]
    vt_ref[...] = nn(zt, matrix(0, blocks))
    vt = vt_ref[...]
    corner = nt(ut, yt)
    zu, vu, inner = nt(zt, ut), nt(vt, ut), nt(zt, vt)
    mine = pl.ds(pl.multiple_of(col * columns, columns), columns)
    ut_c, yt_c, zt_c, vt_c = ut_ref[:, mine], yt_ref[:, mine], zt_ref[:, mine], vt_ref[:, mine]
    wt_c = 2.0 * yt_c - 2.0 * tn(corner, ut_c)
    panel_c = zt_c - 2.0 * nn(zu, ut_c)
    moved_c = vt_c - 2.0 * nn(vu, ut_c)
    rows = whole(a_ref[:, row])
    u_r = nt(rows[:, :B], inverse)
    y_r = nt(rows, ut)
    w_r = 2.0 * y_r - 2.0 * nn(u_r, corner)
    panel_r = rows[:, later] - 2.0 * nn(y_r, ut_ref[:, later]) - 2.0 * nt(u_r, zu)
    moved_r = nt(rows, zt) - 2.0 * nt(u_r, vu)
    result = whole(h_ref[...]) - nn(u_r, wt_c) - nn(w_r, ut_c)

    inverse = second_ref[...]
    both = tn(inverse, nn(inverse, jnp.concatenate([panel_c, moved_c], axis=1)))
    solved, image = both[:, :columns], both[:, columns:]
    bent = nn(inner, solved)
    image = image - 2.0 * tn(inverse, nn(inverse, bent))
    result = result - 2.0 * nn(panel_r, image) - 2.0 * nn(moved_r, solved)
    out_ref[...] = result.reshape(out_ref.shape)

    for stage, source, (slot, d, piece, peer) in sent:
        def action(stage=stage, slot=slot, d=d, piece=piece, peer=peer):
            copy(stage, slot, d, piece, peer).wait_send()

        guarded(stage, source, action)


def local_fast(hamiltonian):
    blocks, strip, columns = hamiltonian.shape
    rows, cols = lax.axis_size("row"), lax.axis_size("col")
    order = blocks * columns
    owners = B // columns
    kept = (blocks - owners) // 2 + 1
    chain = cols // 2
    vmem = pl.BlockSpec(memory_space=pltpu.VMEM)
    return pl.pallas_call(
        panels_kernel,
        out_shape=jax.ShapeDtypeStruct(hamiltonian.shape, jnp.float32),
        in_specs=[vmem],
        out_specs=vmem,
        scratch_shapes=[
            pltpu.VMEM((blocks, rows, strip, order), jnp.float32),
            pltpu.VMEM((cols, rows // 2, 2, owners, strip, columns), jnp.float32),
            pltpu.VMEM((cols, rows // 2, 2, kept, strip, columns), jnp.float32),
            pltpu.VMEM((B, 2 * B), jnp.float32),
            pltpu.VMEM((B, B), jnp.float32),
            pltpu.VMEM((B, B), jnp.float32),
            pltpu.VMEM((B, order), jnp.float32),
            pltpu.VMEM((B, order), jnp.float32),
            pltpu.VMEM((B, order), jnp.float32),
            pltpu.VMEM((B, order), jnp.float32),
            pltpu.SemaphoreType.DMA((12 * chain,)),
            pltpu.SemaphoreType.DMA((12 * chain,)),
        ],
        compiler_params=pltpu.CompilerParams(
            collective_id=0, has_side_effects=True, vmem_limit_bytes=56 * 1024 * 1024
        ),
        cost_estimate=pl.CostEstimate(
            flops=180 * B**3, bytes_accessed=8 * blocks * strip * columns, transcendentals=0
        ),
    )(hamiltonian)


def from_root(block, axis, source):
    block = jnp.where(lax.axis_index(axis) == source, block, jnp.zeros_like(block))
    return lax.psum(block, axis)


def flat_rows(blocked):
    return blocked.reshape(-1, blocked.shape[-1])


def transposed_product(left_rows, right_rows):
    return jnp.dot(left_rows.T, right_rows, precision=HIGHEST, preferred_element_type=jnp.float32)


def outer_blocks(blocked, column_rows):
    return jnp.einsum("ajp,kp->ajk", blocked, column_rows, precision=HIGHEST)


def local_shared(hamiltonian):
    blocks, strip, columns = hamiltonian.shape
    col_index = lax.axis_index("col")
    owners_each = B // columns
    matrix = hamiltonian
    first_portions = []
    for owner_step in range(2 * owners_each):
        first_portions.append(from_root(hamiltonian, "col", owner_step))
    early_panels = jnp.concatenate(first_portions, axis=2)
    next_panel = early_panels[:, :, B : 2 * B]
    for panel_index in range(2):
        if panel_index == 0:
            panel_blocks = early_panels[:, :, 0:B]
        else:
            panel_blocks = next_panel
        panel_rows = flat_rows(panel_blocks)
        gram_matrix = lax.psum(transposed_product(panel_rows, panel_rows), "row")
        factor = jnp.linalg.cholesky(gram_matrix)
        reflector = lax.linalg.triangular_solve(
            factor, panel_rows, left_side=False, lower=True, transpose_a=True
        )
        reflector_blocks = reflector.reshape(blocks, strip, B)
        partial_image = transposed_product(flat_rows(matrix), reflector)
        image_piece = lax.psum_scatter(partial_image, "row", scatter_dimension=0, tiled=True)
        own_reflector = lax.dynamic_index_in_dim(reflector_blocks, col_index, 0, keepdims=False)
        reflector_cols, shared_cols = (
            lax.all_gather(own_reflector, "row", axis=0, tiled=True),
            lax.all_gather(image_piece, "row", axis=0, tiled=True),
        )
        product_own = None
        image_rows = lax.all_gather(image_piece[None], "col", axis=0, tiled=True)
        corner = lax.psum(transposed_product(reflector, flat_rows(image_rows)), "row")
        corrected = 2.0 * image_rows - 2.0 * jnp.einsum(
            "ajp,pq->ajq", reflector_blocks, corner, precision=HIGHEST
        )
        corrected_cols = 2.0 * shared_cols - 2.0 * jnp.dot(
            reflector_cols, corner, precision=HIGHEST, preferred_element_type=jnp.float32
        )
        matrix = (
            matrix
            - outer_blocks(reflector_blocks, corrected_cols)
            - outer_blocks(corrected, reflector_cols)
        )
        product_own = corrected
        if panel_index == 0:
            basis_next = reflector_blocks[owners_each : 2 * owners_each]
            product_next = product_own[owners_each : 2 * owners_each]
            basis_gathered, product_gathered = (
                lax.all_gather(basis_next, "row", axis=1, tiled=True),
                lax.all_gather(product_next, "row", axis=1, tiled=True),
            )
            next_panel = (
                next_panel
                - outer_blocks(reflector_blocks, flat_rows(product_gathered))
                - outer_blocks(product_own, flat_rows(basis_gathered))
            )
    return matrix


def local(hamiltonian):
    blocks, strip, columns = hamiltonian.shape
    rows, cols = lax.axis_size("row"), lax.axis_size("col")
    owners = B // columns
    fits = blocks * columns <= FAST_ORDER and rows == 4 and cols == blocks and rows * strip == columns
    even = cols % 2 == 0 and owners % 2 == 0 and (blocks - owners) // 2 % 2 == 1
    if fits and even:
        return local_fast(hamiltonian)
    return local_shared(hamiltonian)


def solution(mesh):
    placed = (P(None, "row", "col"),)
    return jax.shard_map(
        local, mesh=mesh, in_specs=placed, out_specs=P(None, "row", "col"), check_vma=False
    )
```

```python
import functools

import jax
import jax.numpy as jnp
from jax import lax
from jax.experimental import pallas as pl
from jax.experimental.pallas import tpu as pltpu
from jax.sharding import PartitionSpec as P

B = 256
NB = 32
GROUP = 16
LANES = 128
FAST_ORDER = 1024
HIGHEST = lax.Precision.HIGHEST
MESH = pl.DeviceIdType.MESH


def dot(left, right, dims, precision=HIGHEST):
    return lax.dot_general(
        left, right, (dims, ((), ())), precision=precision, preferred_element_type=jnp.float32
    )


def nn(left, right, precision=HIGHEST):
    return dot(left, right, ((1,), (0,)), precision)


def nt(left, right, precision=HIGHEST):
    return dot(left, right, ((1,), (1,)), precision)


def tn(left, right, precision=HIGHEST):
    return dot(left, right, ((0,), (0,)), precision)


def split2(value):
    high = value.astype(jnp.bfloat16)
    return high, (value - high.astype(jnp.float32)).astype(jnp.bfloat16)


def split3(value):
    high = value.astype(jnp.bfloat16)
    value = value - high.astype(jnp.float32)
    return (high, *split2(value))


def stacked(left, right, dims):
    left = jnp.concatenate(left, axis=dims[0][0])
    right = jnp.concatenate(right, axis=dims[1][0])
    return lax.dot_general(left, right, (dims, ((), ())), preferred_element_type=jnp.float32)


def product(left, right, dims):
    return stacked((left[0], left[0], left[1]), (right[0], right[1], right[0]), dims)


NN = ((1,), (0,))
NT = ((1,), (1,))
TN = ((0,), (0,))


def gram_matrix(value):
    a, b, c = split3(value)
    mixed = stacked((a, a), (b, c), NT)
    return stacked((a, b), (a, b), NT) + (mixed + mixed.T)


def wide(value, times):
    return value if times == 1 else jnp.concatenate([value] * times, axis=1)


def inverse_factor(gram, work_ref, out_ref, tick):
    size = gram.shape[0]
    work_ref[:, :size] = gram
    work_ref[:, size:] = (
        lax.broadcasted_iota(jnp.int32, (size, size), 0)
        == lax.broadcasted_iota(jnp.int32, (size, size), 1)
    ).astype(jnp.float32)
    out_ref[...] = jnp.zeros((size, size), jnp.float32)
    for low in range(0, size, NB):
        high = low + NB
        first = low // LANES * LANES
        last = size + -(-high // LANES) * LANES
        times = (last - first) // LANES
        rows = work_ref[low:high, first:last]
        done = []
        for start in range(0, NB, GROUP):
            lane = low + start - first
            height = NB - start
            columns = [
                jnp.broadcast_to(rows[:, lane + c : lane + c + 1], (height, LANES))
                for c in range(GROUP)
            ]
            ids = lax.broadcasted_iota(jnp.int32, (height, LANES), 0)
            pivots = jnp.ones((GROUP, LANES), jnp.float32)
            for k in range(GROUP):
                pivot = columns[k][k : k + 1]
                pivots = jnp.where(ids[:GROUP] == k, pivot, pivots)
                if start + k == NB - 1:
                    break
                below = jnp.where(ids > k, columns[k], 0.0) * (1.0 / pivot)
                for c in range(k + 1, GROUP):
                    columns[c] = columns[c] - below * columns[c][k : k + 1]
                rows = rows - wide(below, times) * rows[k : k + 1]
                tick(low + start + k)
            done.append(rows[:GROUP] * wide(lax.rsqrt(pivots), times))
            rows = rows[GROUP:]
        rows = jnp.concatenate(done, axis=0)
        out_ref[low:high, : last - size] = rows[:, size - first :]
        if high < size:
            base = high // LANES * LANES
            a, b, c = split3(rows)
            right = (a, b, a, b, c, a)
            left = [part[:, base - first : size - first] for part in (a, a, b, b, a, c)]
            update = stacked(left, right, TN)
            work_ref[high:, first:last] -= update[high - base :]


def panels_kernel(
    h_ref, out_ref, a_ref, high_ref, low_ref, first_ref, rest_ref, work_ref, inverse_ref, second_ref,
    part_ref, product_ref, send_sems, recv_sems,
):
    blocks, strip, columns = h_ref.shape
    chain = lax.axis_size("col") // 2
    order = blocks * columns
    owners = B // columns
    others = blocks - owners
    kept = rest_ref.shape[3]
    row = lax.axis_index("row")
    col = lax.axis_index("col")
    x, core = row // 2, row % 2
    z, y = col // 2, col % 2
    over_core = (x * 2 + 1 - core, col)
    plane = [
        ((1 - x) * 2 + core, z * 2 + 1 - y),
        ((1 - x) * 2 + core, col),
        (row, z * 2 + 1 - y),
    ]
    corners = [(1 - x, 1 - y), (1 - x, y), (x, 1 - y)]

    def along_z(d):
        return (row, lax.rem(z + d, chain) * 2 + y)

    barrier = pltpu.get_barrier_semaphore()
    peers = [along_z(d) for d in range(1, chain)] + plane + [over_core]
    for peer in peers:
        pl.semaphore_signal(barrier, inc=1, device_id=peer, device_id_type=MESH)

    first_ref[col, x, core] = h_ref[:owners]

    @pl.when(col >= owners)
    def _():
        for i in range(kept):
            rest_ref[col, x, core, i] = h_ref[owners + lax.rem(col - owners + i, others)]

    pl.semaphore_wait(barrier, len(peers))

    per_stage = 5 * chain
    buffers = (first_ref, rest_ref)
    sent = []

    def copy(stage, slot, d, piece, peer):
        index = stage * per_stage + slot * chain + d
        return pltpu.make_async_remote_copy(
            src_ref=piece,
            dst_ref=piece,
            send_sem=send_sems.at[index],
            recv_sem=recv_sems.at[index],
            device_id=peer,
            device_id_type=MESH,
        )

    def guarded(stage, source, action):
        if stage == 0:
            action()
        else:
            pl.when(source >= owners // 2)(action)

    def transfer(stage, d, phase):
        ref = buffers[stage]
        source = lax.rem(z + chain - d, chain)
        launches = []

        def here(px, py):
            return ref.at[source * 2 + py, px, core]

        if phase == 1:
            launches = [(1 + n, here(x, y), peer) for n, peer in enumerate(plane)]
        elif phase == 2:
            launches = [(4, ref.at[pl.ds(source * 2, 2), pl.ds(0, 2), core], over_core)]

        def action():
            if phase == 1 and d > 0:
                copy(stage, 0, d, here(x, y), along_z(d)).wait_recv()
            elif phase == 2:
                for n, (corner, peer) in enumerate(zip(corners, plane)):
                    copy(stage, 1 + n, d, here(*corner), peer).wait_recv()
            elif phase == 3:
                piece = ref.at[pl.ds(source * 2, 2), pl.ds(0, 2), 1 - core]
                copy(stage, 4, d, piece, over_core).wait_recv()
            for slot, piece, peer in launches:
                copy(stage, slot, d, piece, peer).start()

        guarded(stage, source, action)
        for slot, piece, peer in launches:
            sent.append((stage, source, (slot, d, piece, peer)))

    def start_z(stage):
        launches = [(0, d, buffers[stage].at[col, x, core], along_z(d)) for d in range(1, chain)]

        def action():
            for launch in launches:
                copy(stage, *launch).start()

        guarded(stage, z, action)
        for launch in launches:
            sent.append((stage, z, launch))

    def finish():
        for stage, source, launch in sent:

            def action(stage=stage, launch=launch):
                copy(stage, *launch).wait_send()

            guarded(stage, source, action)

    def whole(block):
        return block.reshape(-1, block.shape[-1])

    def rows_of(ref, low, high):
        return ref[low * columns : high * columns]

    def place(block_row, block_col, block):
        lanes = slice(block_col * columns, (block_col + 1) * columns)
        down = slice(block_row * columns, (block_row + 1) * columns)
        a_ref[block_row, :, :, lanes] = block.reshape(-1, strip, columns)
        high_ref[down, lanes], low_ref[down, lanes] = split2(block)

    def matrix(low, high):
        return whole(whole(a_ref[low:high]).reshape(-1, order))

    start_z(0)
    transfer(0, 0, 1)
    start_z(1)
    for d in range(1, chain):
        transfer(0, d, 1)
    transfer(1, 0, 1)
    for d in range(chain):
        transfer(0, d, 2)
    transfer(1, 1, 1)
    for d in range(chain):
        transfer(0, d, 3)
    for c in range(blocks):
        for i in range(owners):
            block = whole(first_ref[c, :, :, i].reshape(-1, strip, columns))
            place(i, c, block)
            if c >= owners:
                place(c, i, block.T)
    gram = gram_matrix(matrix(0, owners))
    work_ref[:, :B] = gram
    first_product = split2(gram)
    moves = {16: (2, 1), 48: (0, 2), 64: (3, 1), 96: (1, 2), 128: (2, 2), 160: (3, 2)}

    def tick_one(pivot):
        if pivot in moves:
            transfer(1, *moves[pivot])

    inverse_factor(gram, work_ref, inverse_ref, tick_one)
    for d in range(chain):
        transfer(1, d, 3)
    for c in range(owners, blocks):
        for i in range(kept):
            a = owners + (c - owners + i) % others
            block = whole(rest_ref[c, :, :, i].reshape(-1, strip, columns))
            place(a, c, block)
            if i > 0 and 2 * i != others:
                place(c, a, block.T)
    TT, YT, UT, ZT, VT = range(5)

    def keep(slot, value, lanes=slice(None)):
        part_ref[slot, 0, :, lanes], part_ref[slot, 1, :, lanes] = split2(value)

    def parts(slot, lanes=slice(None)):
        return part_ref[slot, 0, :, lanes], part_ref[slot, 1, :, lanes]

    def joined(slot, lanes):
        high, low = parts(slot, lanes)
        return high.astype(jnp.float32) + low.astype(jnp.float32)

    def a_parts(down, lanes):
        return high_ref[down, lanes], low_ref[down, lanes]

    every, early, later = slice(0, order), slice(0, B), slice(B, 2 * B)
    panel = a_parts(early, every)
    part_ref[TT, 0, :, early], part_ref[TT, 1, :, early] = first_product
    keep(TT, product(panel, a_parts(every, slice(B, order)), NN), slice(B, order))
    inverse = split2(inverse_ref[...])
    keep(YT, product(inverse, parts(TT), NN))
    keep(UT, product(inverse, panel, NN))
    zt = matrix(owners, 2 * owners) - 2.0 * product(parts(UT, later), parts(YT), TN)
    keep(ZT, zt)
    gram = gram_matrix(zt)

    mine = pl.ds(pl.multiple_of(col * columns, columns), columns)
    held = {}

    def fill_rows():
        held["rows"] = split2(whole(a_ref[:, row]))

    def fill_corner():
        held["corner"] = split2(product(parts(UT), parts(YT), NT))

    def fill_zu():
        held["zu"] = split2(product(parts(ZT), parts(UT), NT))

    def fill_vu():
        held["vu"] = split2(product(parts(ZT), parts(YT), NT))

    def fill_v(n):
        lanes = slice(n * columns, (n + 1) * columns)
        keep(VT, product(parts(ZT), a_parts(every, lanes), NN), lanes)

    def fill_inner():
        held["inner"] = split2(product(parts(ZT), parts(VT), NT))

    def fill_columns():
        ut_c = parts(UT, mine)
        held["wt_c"] = 2.0 * joined(YT, mine) - 2.0 * product(held["corner"], ut_c, TN)
        held["panel_c"] = joined(ZT, mine) - 2.0 * product(held["zu"], ut_c, NN)
        held["moved_c"] = joined(VT, mine) - 2.0 * product(held["vu"], ut_c, NN)

    def fill_rows_u():
        first = tuple(part[:, :B] for part in held["rows"])
        held["u_r"] = split2(product(first, inverse, NT))

    def fill_rows_y():
        held["y_r"] = product(held["rows"], parts(UT), NT)

    def fill_rows_v():
        held["v_r"] = product(held["rows"], parts(ZT), NT)

    def fill_rows_rest():
        u_r, y_r = held["u_r"], held["y_r"]
        held["w_r"] = split2(2.0 * y_r - 2.0 * product(u_r, held["corner"], NN))
        panel_r = whole(a_ref[:, row])[:, later] - 2.0 * product(split2(y_r), parts(UT, later), NN)
        held["panel_r"] = split2(panel_r - 2.0 * product(u_r, held["zu"], NT))
        held["moved_r"] = split2(held["v_r"] - 2.0 * product(u_r, held["vu"], NT))

    def fill_result():
        total = product(held["u_r"], split2(held["wt_c"]), NN)
        product_ref[...] = total + product(held["w_r"], parts(UT, mine), NN)

    fillers = [fill_rows, fill_corner, fill_zu, fill_vu, fill_rows_u, fill_rows_y, fill_rows_v, fill_rows_rest]
    fillers += [functools.partial(fill_v, n) for n in range(blocks)]
    fillers += [fill_inner, fill_columns, fill_result]
    spacing = 12

    def tick_two(pivot):
        if spacing and pivot % spacing == 3 and fillers:
            fillers.pop(0)()

    inverse_factor(gram, work_ref, second_ref, tick_two)
    while fillers:
        fillers.pop(0)()
    inverse = split2(second_ref[...])
    both = split2(jnp.concatenate([held["panel_c"], held["moved_c"]], axis=1))
    both = product(inverse, split2(product(inverse, both, NN)), TN)
    solved, image = split2(both[:, :columns]), both[:, columns:]
    bent = split2(product(held["inner"], solved, NN))
    image = image - 2.0 * product(inverse, split2(product(inverse, bent, NN)), TN)
    update = product(held["panel_r"], split2(image), NN) + product(held["moved_r"], solved, NN)
    out_ref[...] = (product_ref[...] + 2.0 * update).reshape(out_ref.shape)
    finish()


def local_fast(hamiltonian):
    blocks, strip, columns = hamiltonian.shape
    rows, cols = lax.axis_size("row"), lax.axis_size("col")
    order = blocks * columns
    owners = B // columns
    kept = (blocks - owners) // 2 + 1
    chain = cols // 2
    vmem = pl.BlockSpec(memory_space=pltpu.VMEM)
    update = pl.pallas_call(
        panels_kernel,
        out_shape=jax.ShapeDtypeStruct(hamiltonian.shape, jnp.float32),
        in_specs=[vmem],
        out_specs=vmem,
        scratch_shapes=[
            pltpu.VMEM((blocks, rows, strip, order), jnp.float32),
            pltpu.VMEM((order, order), jnp.bfloat16),
            pltpu.VMEM((order, order), jnp.bfloat16),
            pltpu.VMEM((cols, rows // 2, 2, owners, strip, columns), jnp.float32),
            pltpu.VMEM((cols, rows // 2, 2, kept, strip, columns), jnp.float32),
            pltpu.VMEM((B, 2 * B), jnp.float32),
            pltpu.VMEM((B, B), jnp.float32),
            pltpu.VMEM((B, B), jnp.float32),
            pltpu.VMEM((5, 2, B, order), jnp.bfloat16),
            pltpu.VMEM((blocks * strip, columns), jnp.float32),
            pltpu.SemaphoreType.DMA((10 * chain,)),
            pltpu.SemaphoreType.DMA((10 * chain,)),
        ],
        compiler_params=pltpu.CompilerParams(
            collective_id=0, has_side_effects=True, vmem_limit_bytes=56 * 1024 * 1024
        ),
        cost_estimate=pl.CostEstimate(
            flops=180 * B**3, bytes_accessed=8 * blocks * strip * columns, transcendentals=0
        ),
    )(hamiltonian)
    return hamiltonian - update


def from_root(block, axis, source):
    block = jnp.where(lax.axis_index(axis) == source, block, jnp.zeros_like(block))
    return lax.psum(block, axis)


def flat_rows(blocked):
    return blocked.reshape(-1, blocked.shape[-1])


def transposed_product(left_rows, right_rows):
    return jnp.dot(left_rows.T, right_rows, precision=HIGHEST, preferred_element_type=jnp.float32)


def outer_blocks(blocked, column_rows):
    return jnp.einsum("ajp,kp->ajk", blocked, column_rows, precision=HIGHEST)


def local_shared(hamiltonian):
    blocks, strip, columns = hamiltonian.shape
    col_index = lax.axis_index("col")
    owners_each = B // columns
    matrix = hamiltonian
    first_portions = []
    for owner_step in range(2 * owners_each):
        first_portions.append(from_root(hamiltonian, "col", owner_step))
    early_panels = jnp.concatenate(first_portions, axis=2)
    next_panel = early_panels[:, :, B : 2 * B]
    for panel_index in range(2):
        if panel_index == 0:
            panel_blocks = early_panels[:, :, 0:B]
        else:
            panel_blocks = next_panel
        panel_rows = flat_rows(panel_blocks)
        gram_matrix = lax.psum(transposed_product(panel_rows, panel_rows), "row")
        factor = jnp.linalg.cholesky(gram_matrix)
        reflector = lax.linalg.triangular_solve(
            factor, panel_rows, left_side=False, lower=True, transpose_a=True
        )
        reflector_blocks = reflector.reshape(blocks, strip, B)
        partial_image = transposed_product(flat_rows(matrix), reflector)
        image_piece = lax.psum_scatter(partial_image, "row", scatter_dimension=0, tiled=True)
        own_reflector = lax.dynamic_index_in_dim(reflector_blocks, col_index, 0, keepdims=False)
        reflector_cols, shared_cols = (
            lax.all_gather(own_reflector, "row", axis=0, tiled=True),
            lax.all_gather(image_piece, "row", axis=0, tiled=True),
        )
        product_own = None
        image_rows = lax.all_gather(image_piece[None], "col", axis=0, tiled=True)
        corner = lax.psum(transposed_product(reflector, flat_rows(image_rows)), "row")
        corrected = 2.0 * image_rows - 2.0 * jnp.einsum(
            "ajp,pq->ajq", reflector_blocks, corner, precision=HIGHEST
        )
        corrected_cols = 2.0 * shared_cols - 2.0 * jnp.dot(
            reflector_cols, corner, precision=HIGHEST, preferred_element_type=jnp.float32
        )
        matrix = (
            matrix
            - outer_blocks(reflector_blocks, corrected_cols)
            - outer_blocks(corrected, reflector_cols)
        )
        product_own = corrected
        if panel_index == 0:
            basis_next = reflector_blocks[owners_each : 2 * owners_each]
            product_next = product_own[owners_each : 2 * owners_each]
            basis_gathered, product_gathered = (
                lax.all_gather(basis_next, "row", axis=1, tiled=True),
                lax.all_gather(product_next, "row", axis=1, tiled=True),
            )
            next_panel = (
                next_panel
                - outer_blocks(reflector_blocks, flat_rows(product_gathered))
                - outer_blocks(product_own, flat_rows(basis_gathered))
            )
    return matrix


def local(hamiltonian):
    blocks, strip, columns = hamiltonian.shape
    rows, cols = lax.axis_size("row"), lax.axis_size("col")
    owners = B // columns
    fits = blocks * columns <= FAST_ORDER and rows == 4 and cols == blocks and rows * strip == columns
    even = cols % 2 == 0 and owners % 2 == 0 and (blocks - owners) // 2 % 2 == 1
    if fits and even:
        return local_fast(hamiltonian)
    return local_shared(hamiltonian)


def solution(mesh):
    placed = (P(None, "row", "col"),)
    return jax.shard_map(
        local, mesh=mesh, in_specs=placed, out_specs=P(None, "row", "col"), check_vma=False
    )
```

```python
import functools

import jax
import jax.numpy as jnp
from jax import lax
from jax.experimental import pallas as pl
from jax.experimental.pallas import tpu as pltpu
from jax.sharding import PartitionSpec as P

B = 256
NB = 32
GROUP = 16
LANES = 128
FAST_ORDER = 1024
HIGHEST = lax.Precision.HIGHEST
MESH = pl.DeviceIdType.MESH


def dot(left, right, dims, precision=HIGHEST):
    return lax.dot_general(
        left, right, (dims, ((), ())), precision=precision, preferred_element_type=jnp.float32
    )


def nn(left, right, precision=HIGHEST):
    return dot(left, right, ((1,), (0,)), precision)


def nt(left, right, precision=HIGHEST):
    return dot(left, right, ((1,), (1,)), precision)


def tn(left, right, precision=HIGHEST):
    return dot(left, right, ((0,), (0,)), precision)


def split2(value):
    high = value.astype(jnp.bfloat16)
    return high, (value - high.astype(jnp.float32)).astype(jnp.bfloat16)


def split3(value):
    high = value.astype(jnp.bfloat16)
    value = value - high.astype(jnp.float32)
    return (high, *split2(value))


def stacked(left, right, dims):
    left = jnp.concatenate(left, axis=dims[0][0])
    right = jnp.concatenate(right, axis=dims[1][0])
    return lax.dot_general(left, right, (dims, ((), ())), preferred_element_type=jnp.float32)


def product(left, right, dims):
    return stacked((left[0], left[0], left[1]), (right[0], right[1], right[0]), dims)


NN = ((1,), (0,))
NT = ((1,), (1,))
TN = ((0,), (0,))


def gram_matrix(value):
    a, b, c = split3(value)
    mixed = stacked((a, a), (b, c), NT)
    return stacked((a, b), (a, b), NT) + (mixed + mixed.T)


def wide(value, times):
    return value if times == 1 else jnp.concatenate([value] * times, axis=1)


def inverse_factor(gram, work_ref, out_ref, tick):
    size = gram.shape[0]
    work_ref[:, :size] = gram
    work_ref[:, size:] = (
        lax.broadcasted_iota(jnp.int32, (size, size), 0)
        == lax.broadcasted_iota(jnp.int32, (size, size), 1)
    ).astype(jnp.float32)
    out_ref[...] = jnp.zeros((size, size), jnp.float32)
    for low in range(0, size, NB):
        high = low + NB
        first = low // LANES * LANES
        last = size + -(-high // LANES) * LANES
        times = (last - first) // LANES
        rows = work_ref[low:high, first:last]
        done = []
        for start in range(0, NB, GROUP):
            lane = low + start - first
            height = NB - start
            columns = [
                jnp.broadcast_to(rows[:, lane + c : lane + c + 1], (height, LANES))
                for c in range(GROUP)
            ]
            ids = lax.broadcasted_iota(jnp.int32, (height, LANES), 0)
            pivots = jnp.ones((GROUP, LANES), jnp.float32)
            for k in range(GROUP):
                pivot = columns[k][k : k + 1]
                pivots = jnp.where(ids[:GROUP] == k, pivot, pivots)
                if start + k == NB - 1:
                    break
                below = jnp.where(ids > k, columns[k], 0.0) * (1.0 / pivot)
                for c in range(k + 1, GROUP):
                    columns[c] = columns[c] - below * columns[c][k : k + 1]
                rows = rows - wide(below, times) * rows[k : k + 1]
                tick(low + start + k)
            done.append(rows[:GROUP] * wide(lax.rsqrt(pivots), times))
            rows = rows[GROUP:]
        rows = jnp.concatenate(done, axis=0)
        out_ref[low:high, : last - size] = rows[:, size - first :]
        if high < size:
            base = high // LANES * LANES
            a, b, c = split3(rows)
            right = (a, b, a, b, c, a)
            left = [part[:, base - first : size - first] for part in (a, a, b, b, a, c)]
            update = stacked(left, right, TN)
            work_ref[high:, first:last] -= update[high - base :]


def panels_kernel(
    h_ref, out_ref, a_ref, high_ref, low_ref, first_ref, rest_ref, work_ref, inverse_ref, second_ref,
    part_ref, product_ref, send_sems, recv_sems,
):
    blocks, strip, columns = h_ref.shape
    chain = lax.axis_size("col") // 2
    order = blocks * columns
    owners = B // columns
    others = blocks - owners
    kept = rest_ref.shape[3]
    row = lax.axis_index("row")
    col = lax.axis_index("col")
    x, core = row // 2, row % 2
    z, y = col // 2, col % 2
    over_core = (x * 2 + 1 - core, col)
    plane = [
        ((1 - x) * 2 + core, z * 2 + 1 - y),
        ((1 - x) * 2 + core, col),
        (row, z * 2 + 1 - y),
    ]
    corners = [(1 - x, 1 - y), (1 - x, y), (x, 1 - y)]

    def along_z(d):
        return (row, lax.rem(z + d, chain) * 2 + y)

    barrier = pltpu.get_barrier_semaphore()
    peers = [along_z(d) for d in range(1, chain)] + plane + [over_core]
    for peer in peers:
        pl.semaphore_signal(barrier, inc=1, device_id=peer, device_id_type=MESH)

    first_ref[col, x, core] = h_ref[:owners]

    @pl.when(col >= owners)
    def _():
        for i in range(kept):
            rest_ref[col, x, core, i] = h_ref[owners + lax.rem(col - owners + i, others)]

    pl.semaphore_wait(barrier, len(peers))

    per_stage = 5 * chain
    buffers = (first_ref, rest_ref)
    sent = []

    def copy(stage, slot, d, piece, peer):
        index = stage * per_stage + slot * chain + d
        return pltpu.make_async_remote_copy(
            src_ref=piece,
            dst_ref=piece,
            send_sem=send_sems.at[index],
            recv_sem=recv_sems.at[index],
            device_id=peer,
            device_id_type=MESH,
        )

    def guarded(stage, source, action):
        if stage == 0:
            action()
        else:
            pl.when(source >= owners // 2)(action)

    def transfer(stage, d, phase):
        ref = buffers[stage]
        source = lax.rem(z + chain - d, chain)
        launches = []

        def here(px, py):
            return ref.at[source * 2 + py, px, core]

        if phase == 1:
            launches = [(1 + n, here(x, y), peer) for n, peer in enumerate(plane)]
        elif phase == 2:
            launches = [(4, ref.at[pl.ds(source * 2, 2), pl.ds(0, 2), core], over_core)]

        def action():
            if phase == 1 and d > 0:
                copy(stage, 0, d, here(x, y), along_z(d)).wait_recv()
            elif phase == 2:
                for n, (corner, peer) in enumerate(zip(corners, plane)):
                    copy(stage, 1 + n, d, here(*corner), peer).wait_recv()
            elif phase == 3:
                piece = ref.at[pl.ds(source * 2, 2), pl.ds(0, 2), 1 - core]
                copy(stage, 4, d, piece, over_core).wait_recv()
            for slot, piece, peer in launches:
                copy(stage, slot, d, piece, peer).start()

        guarded(stage, source, action)
        for slot, piece, peer in launches:
            sent.append((stage, source, (slot, d, piece, peer)))

    def start_z(stage):
        launches = [(0, d, buffers[stage].at[col, x, core], along_z(d)) for d in range(1, chain)]

        def action():
            for launch in launches:
                copy(stage, *launch).start()

        guarded(stage, z, action)
        for launch in launches:
            sent.append((stage, z, launch))

    def finish():
        for stage, source, launch in sent:

            def action(stage=stage, launch=launch):
                copy(stage, *launch).wait_send()

            guarded(stage, source, action)

    def whole(block):
        return block.reshape(-1, block.shape[-1])

    def rows_of(ref, low, high):
        return ref[low * columns : high * columns]

    def place(block_row, block_col, block):
        lanes = slice(block_col * columns, (block_col + 1) * columns)
        down = slice(block_row * columns, (block_row + 1) * columns)
        a_ref[block_row, :, :, lanes] = block.reshape(-1, strip, columns)
        high_ref[down, lanes], low_ref[down, lanes] = split2(block)

    def matrix(low, high):
        return whole(whole(a_ref[low:high]).reshape(-1, order))

    start_z(0)
    transfer(0, 0, 1)
    transfer(1, 0, 1)
    transfer(0, 1, 1)
    start_z(1)
    for d in range(2, chain):
        transfer(0, d, 1)
    for d in range(1, chain):
        transfer(1, d, 1)
    for phase in (2, 3):
        for d in range(chain):
            transfer(0, d, phase)
    for c in range(blocks):
        for i in range(owners):
            block = whole(first_ref[c, :, :, i].reshape(-1, strip, columns))
            place(i, c, block)
            if c >= owners:
                place(c, i, block.T)
    gram = gram_matrix(matrix(0, owners))
    work_ref[:, :B] = gram
    first_product = split2(gram)
    moves = {80: (0, 2), 100: (1, 2), 125: (2, 2), 150: (3, 2)}

    def tick_one(pivot):
        if pivot in moves:
            transfer(1, *moves[pivot])

    inverse_factor(gram, work_ref, inverse_ref, tick_one)
    for d in range(chain):
        transfer(1, d, 3)
    for c in range(owners, blocks):
        for i in range(kept):
            a = owners + (c - owners + i) % others
            block = whole(rest_ref[c, :, :, i].reshape(-1, strip, columns))
            place(a, c, block)
            if i > 0 and 2 * i != others:
                place(c, a, block.T)
    TT, YT, UT, ZT, VT = range(5)

    def keep(slot, value, lanes=slice(None)):
        part_ref[slot, 0, :, lanes], part_ref[slot, 1, :, lanes] = split2(value)

    def parts(slot, lanes=slice(None)):
        return part_ref[slot, 0, :, lanes], part_ref[slot, 1, :, lanes]

    def joined(slot, lanes):
        high, low = parts(slot, lanes)
        return high.astype(jnp.float32) + low.astype(jnp.float32)

    def a_parts(down, lanes):
        return high_ref[down, lanes], low_ref[down, lanes]

    every, early, later = slice(0, order), slice(0, B), slice(B, 2 * B)
    panel = a_parts(early, every)
    part_ref[TT, 0, :, early], part_ref[TT, 1, :, early] = first_product
    keep(TT, product(panel, a_parts(every, slice(B, order)), NN), slice(B, order))
    inverse = split2(inverse_ref[...])
    keep(YT, product(inverse, parts(TT), NN))
    keep(UT, product(inverse, panel, NN))
    zt = matrix(owners, 2 * owners) - 2.0 * product(parts(UT, later), parts(YT), TN)
    keep(ZT, zt)
    gram = gram_matrix(zt)

    mine = pl.ds(pl.multiple_of(col * columns, columns), columns)
    held = {}

    def fill_rows():
        held["rows"] = split2(whole(a_ref[:, row]))

    def fill_corner():
        held["corner"] = split2(product(parts(UT), parts(YT), NT))

    def fill_uz():
        u_later = parts(UT, later)
        held["uz"] = split2(joined(YT, later) - 2.0 * product(held["corner"], u_later, NN))

    def fill_vu():
        held["vu"] = split2(product(parts(ZT), parts(YT), NT))

    def fill_v(n):
        lanes = slice(n * B, (n + 1) * B)
        keep(VT, product(parts(ZT), a_parts(every, lanes), NN), lanes)

    def fill_inner():
        held["inner"] = split2(product(parts(ZT), parts(VT), NT))

    def fill_columns():
        ut_c = parts(UT, mine)
        held["wt_c"] = 2.0 * joined(YT, mine) - 2.0 * product(held["corner"], ut_c, NN)
        panel_c = joined(ZT, mine) - 2.0 * product(held["uz"], ut_c, TN)
        moved_c = joined(VT, mine) - 2.0 * product(held["vu"], ut_c, NN)
        sides = [split2(panel_c), split2(moved_c), held["inner"]]
        held["sides"] = tuple(jnp.concatenate(part, axis=1) for part in zip(*sides))

    def fill_rows_u():
        first = tuple(part[:, :B] for part in held["rows"])
        held["u_r"] = split2(product(first, inverse, NT))

    def fill_rows_y():
        held["y_r"] = product(held["rows"], parts(UT), NT)

    def fill_rows_v():
        held["v_r"] = product(held["rows"], parts(ZT), NT)

    def fill_rows_rest():
        u_r, y_r = held["u_r"], held["y_r"]
        held["w_r"] = split2(2.0 * y_r - 2.0 * product(u_r, held["corner"], NN))
        panel_r = whole(a_ref[:, row])[:, later] - 2.0 * product(split2(y_r), parts(UT, later), NN)
        panel_r = panel_r - 2.0 * product(u_r, held["uz"], NN)
        moved_r = held["v_r"] - 2.0 * product(u_r, held["vu"], NT)
        held["rows_2"] = split2(jnp.concatenate([panel_r, moved_r], axis=0))

    def fill_result():
        left = [jnp.concatenate(pair, axis=1) for pair in zip(held["u_r"], held["w_r"])]
        right = [jnp.concatenate(pair, axis=0) for pair in zip(split2(held["wt_c"]), parts(UT, mine))]
        product_ref[...] = product(left, right, NN)

    fillers = [fill_corner, fill_vu] + [functools.partial(fill_v, n) for n in range(order // B)]
    fillers += [fill_inner, fill_rows, fill_rows_u, fill_uz, fill_rows_y, fill_rows_v, fill_rows_rest]
    fillers += [fill_columns, fill_result]
    spacing = 16

    def tick_two(pivot):
        if spacing and pivot % spacing == 3 and fillers:
            fillers.pop(0)()

    inverse_factor(gram, work_ref, second_ref, tick_two)
    while fillers:
        fillers.pop(0)()
    inverse = split2(second_ref[...])
    mixed = product(inverse, held["sides"], NN)
    rows = product(held["rows_2"], inverse, NT)
    basis_c, moved_c, inner = mixed[:, :columns], mixed[:, columns : 2 * columns], mixed[:, 2 * columns :]
    corner = split2(product(split2(inner), inverse, NT))
    bent = 2.0 * moved_c - 4.0 * product(corner, split2(basis_c), NN)
    right = split2(jnp.concatenate([bent, 2.0 * basis_c], axis=0))
    half = blocks * strip
    left = split2(jnp.concatenate([rows[:half], rows[half:]], axis=1))
    update = product(left, right, NN)
    out_ref[...] = (product_ref[...] + update).reshape(out_ref.shape)
    finish()


def local_fast(hamiltonian):
    blocks, strip, columns = hamiltonian.shape
    rows, cols = lax.axis_size("row"), lax.axis_size("col")
    order = blocks * columns
    owners = B // columns
    kept = (blocks - owners) // 2 + 1
    chain = cols // 2
    vmem = pl.BlockSpec(memory_space=pltpu.VMEM)
    update = pl.pallas_call(
        panels_kernel,
        out_shape=jax.ShapeDtypeStruct(hamiltonian.shape, jnp.float32),
        in_specs=[vmem],
        out_specs=vmem,
        scratch_shapes=[
            pltpu.VMEM((blocks, rows, strip, order), jnp.float32),
            pltpu.VMEM((order, order), jnp.bfloat16),
            pltpu.VMEM((order, order), jnp.bfloat16),
            pltpu.VMEM((cols, rows // 2, 2, owners, strip, columns), jnp.float32),
            pltpu.VMEM((cols, rows // 2, 2, kept, strip, columns), jnp.float32),
            pltpu.VMEM((B, 2 * B), jnp.float32),
            pltpu.VMEM((B, B), jnp.float32),
            pltpu.VMEM((B, B), jnp.float32),
            pltpu.VMEM((5, 2, B, order), jnp.bfloat16),
            pltpu.VMEM((blocks * strip, columns), jnp.float32),
            pltpu.SemaphoreType.DMA((10 * chain,)),
            pltpu.SemaphoreType.DMA((10 * chain,)),
        ],
        compiler_params=pltpu.CompilerParams(
            collective_id=0, has_side_effects=True, vmem_limit_bytes=24 * 1024 * 1024
        ),
        cost_estimate=pl.CostEstimate(
            flops=180 * B**3, bytes_accessed=8 * blocks * strip * columns, transcendentals=0
        ),
    )(hamiltonian)
    return hamiltonian - update


def from_root(block, axis, source):
    block = jnp.where(lax.axis_index(axis) == source, block, jnp.zeros_like(block))
    return lax.psum(block, axis)


def flat_rows(blocked):
    return blocked.reshape(-1, blocked.shape[-1])


def transposed_product(left_rows, right_rows):
    return jnp.dot(left_rows.T, right_rows, precision=HIGHEST, preferred_element_type=jnp.float32)


def outer_blocks(blocked, column_rows):
    return jnp.einsum("ajp,kp->ajk", blocked, column_rows, precision=HIGHEST)


def local_shared(hamiltonian):
    blocks, strip, columns = hamiltonian.shape
    col_index = lax.axis_index("col")
    owners_each = B // columns
    matrix = hamiltonian
    first_portions = []
    for owner_step in range(2 * owners_each):
        first_portions.append(from_root(hamiltonian, "col", owner_step))
    early_panels = jnp.concatenate(first_portions, axis=2)
    next_panel = early_panels[:, :, B : 2 * B]
    for panel_index in range(2):
        if panel_index == 0:
            panel_blocks = early_panels[:, :, 0:B]
        else:
            panel_blocks = next_panel
        panel_rows = flat_rows(panel_blocks)
        gram_matrix = lax.psum(transposed_product(panel_rows, panel_rows), "row")
        factor = jnp.linalg.cholesky(gram_matrix)
        reflector = lax.linalg.triangular_solve(
            factor, panel_rows, left_side=False, lower=True, transpose_a=True
        )
        reflector_blocks = reflector.reshape(blocks, strip, B)
        partial_image = transposed_product(flat_rows(matrix), reflector)
        image_piece = lax.psum_scatter(partial_image, "row", scatter_dimension=0, tiled=True)
        own_reflector = lax.dynamic_index_in_dim(reflector_blocks, col_index, 0, keepdims=False)
        reflector_cols, shared_cols = (
            lax.all_gather(own_reflector, "row", axis=0, tiled=True),
            lax.all_gather(image_piece, "row", axis=0, tiled=True),
        )
        product_own = None
        image_rows = lax.all_gather(image_piece[None], "col", axis=0, tiled=True)
        corner = lax.psum(transposed_product(reflector, flat_rows(image_rows)), "row")
        corrected = 2.0 * image_rows - 2.0 * jnp.einsum(
            "ajp,pq->ajq", reflector_blocks, corner, precision=HIGHEST
        )
        corrected_cols = 2.0 * shared_cols - 2.0 * jnp.dot(
            reflector_cols, corner, precision=HIGHEST, preferred_element_type=jnp.float32
        )
        matrix = (
            matrix
            - outer_blocks(reflector_blocks, corrected_cols)
            - outer_blocks(corrected, reflector_cols)
        )
        product_own = corrected
        if panel_index == 0:
            basis_next = reflector_blocks[owners_each : 2 * owners_each]
            product_next = product_own[owners_each : 2 * owners_each]
            basis_gathered, product_gathered = (
                lax.all_gather(basis_next, "row", axis=1, tiled=True),
                lax.all_gather(product_next, "row", axis=1, tiled=True),
            )
            next_panel = (
                next_panel
                - outer_blocks(reflector_blocks, flat_rows(product_gathered))
                - outer_blocks(product_own, flat_rows(basis_gathered))
            )
    return matrix


def local(hamiltonian):
    blocks, strip, columns = hamiltonian.shape
    rows, cols = lax.axis_size("row"), lax.axis_size("col")
    owners = B // columns
    fits = blocks * columns <= FAST_ORDER and rows == 4 and cols == blocks and rows * strip == columns
    even = cols % 2 == 0 and owners % 2 == 0 and (blocks - owners) // 2 % 2 == 1
    if fits and even:
        return local_fast(hamiltonian)
    return local_shared(hamiltonian)


def solution(mesh):
    placed = (P(None, "row", "col"),)
    return jax.shard_map(
        local, mesh=mesh, in_specs=placed, out_specs=P(None, "row", "col"), check_vma=False
    )
```

```python
import functools

import jax
import jax.numpy as jnp
from jax import lax
from jax.experimental import pallas as pl
from jax.experimental.pallas import tpu as pltpu
from jax.sharding import PartitionSpec as P

B = 256
NB = 32
GROUP = 16
LANES = 128
FAST_ORDER = 1024
HIGHEST = lax.Precision.HIGHEST
MESH = pl.DeviceIdType.MESH


def dot(left, right, dims, precision=HIGHEST):
    return lax.dot_general(
        left, right, (dims, ((), ())), precision=precision, preferred_element_type=jnp.float32
    )


def nn(left, right, precision=HIGHEST):
    return dot(left, right, ((1,), (0,)), precision)


def nt(left, right, precision=HIGHEST):
    return dot(left, right, ((1,), (1,)), precision)


def tn(left, right, precision=HIGHEST):
    return dot(left, right, ((0,), (0,)), precision)


def split2(value):
    high = value.astype(jnp.bfloat16)
    return high, (value - high.astype(jnp.float32)).astype(jnp.bfloat16)


def split3(value):
    high = value.astype(jnp.bfloat16)
    value = value - high.astype(jnp.float32)
    return (high, *split2(value))


def stacked(left, right, dims):
    left = jnp.concatenate(left, axis=dims[0][0])
    right = jnp.concatenate(right, axis=dims[1][0])
    return lax.dot_general(left, right, (dims, ((), ())), preferred_element_type=jnp.float32)


def product(left, right, dims):
    return stacked((left[0], left[0], left[1]), (right[0], right[1], right[0]), dims)


NN = ((1,), (0,))
NT = ((1,), (1,))
TN = ((0,), (0,))


def gram_matrix(value):
    a, b, c = split3(value)
    mixed = stacked((a, a), (b, c), NT)
    return stacked((a, b), (a, b), NT) + (mixed + mixed.T)


def wide(value, times):
    return value if times == 1 else jnp.concatenate([value] * times, axis=1)


def inverse_factor(gram, work_ref, out_ref, tick, between):
    size = gram.shape[0]
    work_ref[:, :size] = gram
    work_ref[:, size:] = (
        lax.broadcasted_iota(jnp.int32, (size, size), 0)
        == lax.broadcasted_iota(jnp.int32, (size, size), 1)
    ).astype(jnp.float32)
    out_ref[...] = jnp.zeros((size, size), jnp.float32)
    for low in range(0, size, NB):
        high = low + NB
        first = low // LANES * LANES
        last = size + -(-high // LANES) * LANES
        times = (last - first) // LANES
        between(low)
        rows = work_ref[low:high, first:last]
        done = []
        for start in range(0, NB, GROUP):
            lane = low + start - first
            height = NB - start
            columns = [
                jnp.broadcast_to(rows[:, lane + c : lane + c + 1], (height, LANES))
                for c in range(GROUP)
            ]
            ids = lax.broadcasted_iota(jnp.int32, (height, LANES), 0)
            pivots = jnp.ones((GROUP, LANES), jnp.float32)
            for k in range(GROUP):
                pivot = columns[k][k : k + 1]
                pivots = jnp.where(ids[:GROUP] == k, pivot, pivots)
                if start + k == NB - 1:
                    break
                under = jnp.where(ids > k, columns[k], 0.0)
                reciprocal = 1.0 / pivot
                if k + 1 < GROUP:
                    columns[k + 1] = columns[k + 1] - under * columns[k + 1][k : k + 1] * reciprocal
                below = under * reciprocal
                for c in range(k + 2, GROUP):
                    columns[c] = columns[c] - below * columns[c][k : k + 1]
                rows = rows - wide(below, times) * rows[k : k + 1]
                tick(low + start + k)
            done.append(rows[:GROUP] * wide(lax.rsqrt(pivots), times))
            rows = rows[GROUP:]
        rows = jnp.concatenate(done, axis=0)
        out_ref[low:high, : last - size] = rows[:, size - first :]
        if high < size:
            base = high // LANES * LANES
            a, b, c = split3(rows)
            right = (a, b, a, b, c, a)
            left = [part[:, base - first : size - first] for part in (a, a, b, b, a, c)]
            update = stacked(left, right, TN)
            work_ref[high:, first:last] -= update[high - base :]


def panels_kernel(
    h_ref, out_ref, a_ref, high_ref, low_ref, first_ref, rest_ref, work_ref, inverse_ref, second_ref,
    part_ref, begun_ref, product_ref, send_sems, recv_sems, own_sems,
):
    blocks, strip, columns = h_ref.shape
    chain = lax.axis_size("col") // 2
    order = blocks * columns
    owners = B // columns
    others = blocks - owners
    kept = rest_ref.shape[3]
    row = lax.axis_index("row")
    col = lax.axis_index("col")
    x, core = row // 2, row % 2
    z, y = col // 2, col % 2
    over_core = (x * 2 + 1 - core, col)
    plane = [
        ((1 - x) * 2 + core, z * 2 + 1 - y),
        ((1 - x) * 2 + core, col),
        (row, z * 2 + 1 - y),
    ]
    corners = [(1 - x, 1 - y), (1 - x, y), (x, 1 - y)]

    def along_z(d):
        return (row, lax.rem(z + d, chain) * 2 + y)

    barrier = pltpu.get_barrier_semaphore()
    peers = [along_z(d) for d in range(1, chain)] + plane + [over_core]
    for peer in peers:
        pl.semaphore_signal(barrier, inc=1, device_id=peer, device_id_type=MESH)

    def own_copies():
        yield pltpu.make_async_copy(h_ref.at[pl.ds(0, owners)], first_ref.at[col, x, core], own_sems.at[0])

    def more_copies():
        for i in range(kept):
            piece = h_ref.at[owners + lax.rem(col - owners + i, others)]
            yield pltpu.make_async_copy(piece, rest_ref.at[col, x, core, i], own_sems.at[1 + i])

    for made in own_copies():
        made.start()

    @pl.when(col >= owners)
    def _():
        for made in more_copies():
            made.start()
        for made in more_copies():
            made.wait()

    for made in own_copies():
        made.wait()
    pl.semaphore_wait(barrier, len(peers))

    short = (owners + others // 2 + 1) // 2
    per_stage = 5 * chain
    buffers = (first_ref, rest_ref)
    sent = []

    def copy(stage, slot, d, piece, peer):
        index = stage * per_stage + slot * chain + d
        return pltpu.make_async_remote_copy(
            src_ref=piece,
            dst_ref=piece,
            send_sem=send_sems.at[index],
            recv_sem=recv_sems.at[index],
            device_id=peer,
            device_id_type=MESH,
        )

    def guarded(stage, source, action):
        count = buffers[stage].shape[3]
        if stage == 0:
            action(pl.ds(0, count))
        else:
            pl.when((source >= owners // 2) & (source < short))(lambda: action(pl.ds(0, count)))
            pl.when(source >= short)(lambda: action(pl.ds(0, count - 1)))

    def transfer(stage, d, phase):
        ref = buffers[stage]
        source = lax.rem(z + chain - d, chain)

        def piece(px, py, part):
            return ref.at[source * 2 + py, px, core, part]

        def both(of_core, part):
            return ref.at[pl.ds(source * 2, 2), pl.ds(0, 2), of_core, part]

        def launches(part):
            if phase == 1:
                return [(1 + n, d, piece(x, y, part), peer) for n, peer in enumerate(plane)]
            return [(4, d, both(core, part), over_core)] if phase == 2 else []

        def action(part):
            if phase == 1 and d > 0:
                copy(stage, 0, d, piece(x, y, part), along_z(d)).wait_recv()
            elif phase == 2:
                for n, (corner, peer) in enumerate(zip(corners, plane)):
                    copy(stage, 1 + n, d, piece(*corner, part), peer).wait_recv()
            elif phase == 3:
                copy(stage, 4, d, both(1 - core, part), over_core).wait_recv()
            for launch in launches(part):
                copy(stage, *launch).start()

        guarded(stage, source, action)
        sent.append((stage, source, launches))

    def start_z(stage):
        def launches(part):
            own = buffers[stage].at[col, x, core, part]
            return [(0, d, own, along_z(d)) for d in range(1, chain)]

        def action(part):
            for launch in launches(part):
                copy(stage, *launch).start()

        guarded(stage, z, action)
        sent.append((stage, z, launches))

    def finish():
        for stage, source, launches in sent:

            def action(part, stage=stage, launches=launches):
                for launch in launches(part):
                    copy(stage, *launch).wait_send()

            guarded(stage, source, action)

    def whole(block):
        return block.reshape(-1, block.shape[-1])

    def rows_of(ref, low, high):
        return ref[low * columns : high * columns]

    def place(block_row, block_col, block):
        lanes = slice(block_col * columns, (block_col + 1) * columns)
        down = slice(block_row * columns, (block_row + 1) * columns)
        a_ref[block_row, :, :, lanes] = block.reshape(-1, strip, columns)
        high_ref[down, lanes], low_ref[down, lanes] = split2(block)

    def matrix(low, high):
        return whole(whole(a_ref[low:high]).reshape(-1, order))

    start_z(0)
    transfer(0, 0, 1)
    transfer(1, 0, 1)
    transfer(0, 1, 1)
    start_z(1)
    for d in range(2, chain):
        transfer(0, d, 1)
    for d in range(1, chain):
        transfer(1, d, 1)
    for phase in (2, 3):
        for d in range(chain):
            transfer(0, d, phase)
    for c in range(blocks):
        for i in range(owners):
            block = whole(first_ref[c, :, :, i].reshape(-1, strip, columns))
            place(i, c, block)
            if c >= owners:
                place(c, i, block.T)
    gram = gram_matrix(matrix(0, owners))
    work_ref[:, :B] = gram
    first_product = split2(gram)
    moves = {192: (0, 1, 2, 3)}

    def onward(low):
        for d in moves.get(low, ()):
            transfer(1, d, 2)

    def nothing(pivot):
        return None

    inverse_factor(gram, work_ref, inverse_ref, nothing, onward)
    onward(B)
    YT, UT, ZT, VT = range(4)

    def keep(slot, value, lanes=slice(None)):
        part_ref[slot, 0, :, lanes], part_ref[slot, 1, :, lanes] = split2(value)

    def parts(slot, lanes=slice(None)):
        return part_ref[slot, 0, :, lanes], part_ref[slot, 1, :, lanes]

    def joined(slot, lanes):
        high, low = parts(slot, lanes)
        return high.astype(jnp.float32) + low.astype(jnp.float32)

    def a_parts(down, lanes):
        return high_ref[down, lanes], low_ref[down, lanes]

    every, early, later, rest = slice(0, order), slice(0, B), slice(B, 2 * B), slice(B, order)
    inverse = split2(inverse_ref[...])
    keep(UT, product(inverse, a_parts(early, every), NN))
    keep(YT, product(inverse, first_product, NN), early)
    begun_ref[...] = product(parts(UT, early), a_parts(early, rest), NN)
    for d in range(chain):
        transfer(1, d, 3)
    for c in range(owners, blocks):
        for i in range(kept):
            a = owners + (c - owners + i) % others
            if i == kept - 1 and c // 2 >= short:
                continue
            block = whole(rest_ref[c, :, :, i].reshape(-1, strip, columns))
            place(a, c, block)
            if i > 0 and (2 * i != others or a // 2 >= short):
                place(c, a, block.T)
    keep(YT, begun_ref[...] + product(parts(UT, rest), a_parts(rest, rest), NN), rest)
    zt = matrix(owners, 2 * owners) - 2.0 * product(parts(UT, later), parts(YT), TN)
    keep(ZT, zt)
    gram = gram_matrix(zt)

    mine = pl.ds(pl.multiple_of(col * columns, columns), columns)
    held = {}

    def fill_rows():
        held["rows"] = split2(whole(a_ref[:, row]))

    def fill_corner():
        held["corner"] = split2(product(parts(UT), parts(YT), NT))

    def fill_uz():
        u_later = parts(UT, later)
        held["uz"] = split2(joined(YT, later) - 2.0 * product(held["corner"], u_later, NN))

    def fill_vu():
        held["vu"] = split2(product(parts(ZT), parts(YT), NT))

    def fill_v(n):
        lanes = slice(n * B, (n + 1) * B)
        if n == 0:
            keep(VT, product(held["uz"], parts(YT, early), TN), lanes)
        else:
            keep(VT, product(parts(ZT), a_parts(every, lanes), NN), lanes)

    def fill_inner():
        held["inner"] = split2(product(parts(ZT), parts(VT), NT))

    def fill_columns():
        ut_c = parts(UT, mine)
        held["wt_c"] = 2.0 * joined(YT, mine) - 2.0 * product(held["corner"], ut_c, NN)
        panel_c = joined(ZT, mine) - 2.0 * product(held["uz"], ut_c, TN)
        moved_c = joined(VT, mine) - 2.0 * product(held["vu"], ut_c, NN)
        sides = [split2(panel_c), split2(moved_c), held["inner"]]
        held["sides"] = tuple(jnp.concatenate(part, axis=1) for part in zip(*sides))

    def fill_rows_u():
        first = tuple(part[:, :B] for part in held["rows"])
        held["u_r"] = split2(product(first, inverse, NT))

    def fill_rows_y():
        held["y_r"] = product(held["rows"], parts(UT), NT)

    def fill_rows_v():
        held["v_r"] = product(held["rows"], parts(ZT), NT)

    def fill_rows_rest():
        u_r, y_r = held["u_r"], held["y_r"]
        held["w_r"] = split2(2.0 * y_r - 2.0 * product(u_r, held["corner"], NN))
        panel_r = whole(a_ref[:, row])[:, later] - 2.0 * product(split2(y_r), parts(UT, later), NN)
        panel_r = panel_r - 2.0 * product(u_r, held["uz"], NN)
        moved_r = held["v_r"] - 2.0 * product(u_r, held["vu"], NT)
        held["rows_2"] = split2(jnp.concatenate([panel_r, moved_r], axis=0))

    def fill_result():
        left = [jnp.concatenate(pair, axis=1) for pair in zip(held["u_r"], held["w_r"])]
        right = [jnp.concatenate(pair, axis=0) for pair in zip(split2(held["wt_c"]), parts(UT, mine))]
        product_ref[...] = product(left, right, NN)

    fillers = [fill_corner, fill_vu, fill_uz] + [functools.partial(fill_v, n) for n in range(order // B)]
    fillers += [fill_inner, fill_rows, fill_rows_u, fill_rows_y, fill_rows_v, fill_rows_rest]
    fillers += [fill_columns, fill_result]
    spacing = 16

    def tick_two(pivot):
        if spacing and pivot % spacing == 3 and fillers:
            fillers.pop(0)()

    inverse_factor(gram, work_ref, second_ref, tick_two, nothing)
    while fillers:
        fillers.pop(0)()
    inverse = split2(second_ref[...])
    mixed = product(inverse, held["sides"], NN)
    rows = product(held["rows_2"], inverse, NT)
    basis_c, moved_c, inner = mixed[:, :columns], mixed[:, columns : 2 * columns], mixed[:, 2 * columns :]
    corner = split2(product(split2(inner), inverse, NT))
    bent = 2.0 * moved_c - 4.0 * product(corner, split2(basis_c), NN)
    right = split2(jnp.concatenate([bent, 2.0 * basis_c], axis=0))
    half = blocks * strip
    left = split2(jnp.concatenate([rows[:half], rows[half:]], axis=1))
    update = product(left, right, NN)
    out_ref[...] = (product_ref[...] + update).reshape(out_ref.shape)
    finish()


def local_fast(hamiltonian):
    blocks, strip, columns = hamiltonian.shape
    rows, cols = lax.axis_size("row"), lax.axis_size("col")
    order = blocks * columns
    owners = B // columns
    kept = (blocks - owners) // 2 + 1
    chain = cols // 2
    vmem = pl.BlockSpec(memory_space=pltpu.VMEM)
    update = pl.pallas_call(
        panels_kernel,
        out_shape=jax.ShapeDtypeStruct(hamiltonian.shape, jnp.float32),
        in_specs=[pl.BlockSpec(memory_space=pltpu.HBM)],
        out_specs=vmem,
        scratch_shapes=[
            pltpu.VMEM((blocks, rows, strip, order), jnp.float32),
            pltpu.VMEM((order, order), jnp.bfloat16),
            pltpu.VMEM((order, order), jnp.bfloat16),
            pltpu.VMEM((cols, rows // 2, 2, owners, strip, columns), jnp.float32),
            pltpu.VMEM((cols, rows // 2, 2, kept, strip, columns), jnp.float32),
            pltpu.VMEM((B, 2 * B), jnp.float32),
            pltpu.VMEM((B, B), jnp.float32),
            pltpu.VMEM((B, B), jnp.float32),
            pltpu.VMEM((4, 2, B, order), jnp.bfloat16),
            pltpu.VMEM((B, order - B), jnp.float32),
            pltpu.VMEM((blocks * strip, columns), jnp.float32),
            pltpu.SemaphoreType.DMA((10 * chain,)),
            pltpu.SemaphoreType.DMA((10 * chain,)),
            pltpu.SemaphoreType.DMA((1 + kept,)),
        ],
        compiler_params=pltpu.CompilerParams(
            collective_id=0, has_side_effects=True, vmem_limit_bytes=24 * 1024 * 1024
        ),
        cost_estimate=pl.CostEstimate(
            flops=180 * B**3, bytes_accessed=8 * blocks * strip * columns, transcendentals=0
        ),
    )(hamiltonian)
    return hamiltonian - update


def from_root(block, axis, source):
    block = jnp.where(lax.axis_index(axis) == source, block, jnp.zeros_like(block))
    return lax.psum(block, axis)


def flat_rows(blocked):
    return blocked.reshape(-1, blocked.shape[-1])


def transposed_product(left_rows, right_rows):
    return jnp.dot(left_rows.T, right_rows, precision=HIGHEST, preferred_element_type=jnp.float32)


def outer_blocks(blocked, column_rows):
    return jnp.einsum("ajp,kp->ajk", blocked, column_rows, precision=HIGHEST)


def local_shared(hamiltonian):
    blocks, strip, columns = hamiltonian.shape
    col_index = lax.axis_index("col")
    owners_each = B // columns
    matrix = hamiltonian
    first_portions = []
    for owner_step in range(2 * owners_each):
        first_portions.append(from_root(hamiltonian, "col", owner_step))
    early_panels = jnp.concatenate(first_portions, axis=2)
    next_panel = early_panels[:, :, B : 2 * B]
    for panel_index in range(2):
        if panel_index == 0:
            panel_blocks = early_panels[:, :, 0:B]
        else:
            panel_blocks = next_panel
        panel_rows = flat_rows(panel_blocks)
        gram_matrix = lax.psum(transposed_product(panel_rows, panel_rows), "row")
        factor = jnp.linalg.cholesky(gram_matrix)
        reflector = lax.linalg.triangular_solve(
            factor, panel_rows, left_side=False, lower=True, transpose_a=True
        )
        reflector_blocks = reflector.reshape(blocks, strip, B)
        partial_image = transposed_product(flat_rows(matrix), reflector)
        image_piece = lax.psum_scatter(partial_image, "row", scatter_dimension=0, tiled=True)
        own_reflector = lax.dynamic_index_in_dim(reflector_blocks, col_index, 0, keepdims=False)
        reflector_cols, shared_cols = (
            lax.all_gather(own_reflector, "row", axis=0, tiled=True),
            lax.all_gather(image_piece, "row", axis=0, tiled=True),
        )
        product_own = None
        image_rows = lax.all_gather(image_piece[None], "col", axis=0, tiled=True)
        corner = lax.psum(transposed_product(reflector, flat_rows(image_rows)), "row")
        corrected = 2.0 * image_rows - 2.0 * jnp.einsum(
            "ajp,pq->ajq", reflector_blocks, corner, precision=HIGHEST
        )
        corrected_cols = 2.0 * shared_cols - 2.0 * jnp.dot(
            reflector_cols, corner, precision=HIGHEST, preferred_element_type=jnp.float32
        )
        matrix = (
            matrix
            - outer_blocks(reflector_blocks, corrected_cols)
            - outer_blocks(corrected, reflector_cols)
        )
        product_own = corrected
        if panel_index == 0:
            basis_next = reflector_blocks[owners_each : 2 * owners_each]
            product_next = product_own[owners_each : 2 * owners_each]
            basis_gathered, product_gathered = (
                lax.all_gather(basis_next, "row", axis=1, tiled=True),
                lax.all_gather(product_next, "row", axis=1, tiled=True),
            )
            next_panel = (
                next_panel
                - outer_blocks(reflector_blocks, flat_rows(product_gathered))
                - outer_blocks(product_own, flat_rows(basis_gathered))
            )
    return matrix


def local(hamiltonian):
    blocks, strip, columns = hamiltonian.shape
    rows, cols = lax.axis_size("row"), lax.axis_size("col")
    owners = B // columns
    fits = blocks * columns <= FAST_ORDER and rows == 4 and cols == blocks and rows * strip == columns
    even = cols % 2 == 0 and owners % 2 == 0 and (blocks - owners) // 2 % 2 == 1
    if fits and even:
        return local_fast(hamiltonian)
    return local_shared(hamiltonian)


def solution(mesh):
    placed = (P(None, "row", "col"),)
    return jax.shard_map(
        local, mesh=mesh, in_specs=placed, out_specs=P(None, "row", "col"), check_vma=False
    )
```
